32 devices in a mesh: seq: 8 (over z, core), res: 4 (over y, x).
Axes of the slice: x: 2, y: 2, z: 4, core: 2. Of those that a mesh axis runs over, the one named last changes fastest.
Arguments:
- pair_grad: bfloat16 [32, 512, 128], P('seq', 'res'), may hold values from -128 to 128
- out_weight: bfloat16 [1024, 128], replicated, may hold values from -0.1875 to 0.1875
- left_feat: bfloat16 [32, 32, 1024], P('res', None, 'seq'), may hold values from -6 to 6
- right_feat: bfloat16 [512, 32, 1024], P('res', None, 'seq'), may hold values from -6 to 6
Outputs:
- grad_left: float32 [32, 32, 1024], P('res', None, 'seq')
- grad_right: float32 [512, 32, 1024], P('res', None, 'seq')
The draws below stay inside these ranges and needn't reach their ends.
All inputs are finite; a program needn't handle non-finite values.
Results may differ from the reference program's by a relative error of at most 0.0029.
Values may be sent and summed in bfloat16 or wider, within the bound.
A program may use at most 64 MiB of HBM per device.

```python
import jax
import jax.numpy as jnp
from jax import lax

C = 32
PAIR = 128
LEFT = 32
PANEL = 8
ROWS = 1024
RIGHT = 512


def spiked(values, stream_key, source, target, blocks, factor):
    owner, partner = [(jnp.arange(values.shape[position]) // (values.shape[position] // blocks)).reshape([-1 if axis == position else 1 for axis in range(values.ndim)]) for position in (source, target)]
    chosen = jax.random.permutation(stream_key, blocks)[partner]
    strong = (owner == chosen) | (owner == (partner + blocks // 2) % blocks)
    return jnp.where(strong, factor * values, values)


def shard_levels(rng, extent, shards, smallest, high):
    factor_of = 1.0
    for axis_at, shards_of in shards:
        heights = jax.random.uniform(jax.random.fold_in(jax.random.fold_in(rng, 6), axis_at), (shards_of,), jnp.float32, smallest / len(shards), high / len(shards))
        factor_of = factor_of * jnp.repeat(jnp.exp(heights), extent[axis_at] // shards_of).reshape((-1,) + (1,) * (len(extent) - 1 - axis_at))
    return factor_of


def scatter_about(key, dims, deviation, reach, shards=(), kind=jnp.bfloat16):
    gain = shard_levels(key, dims, shards, -0.22, 0.18) if shards else 1.0
    array = jax.random.normal(key, dims, jnp.float32) * deviation * gain
    return jnp.minimum(jnp.maximum(array, -reach), reach).astype(kind)


def gaussian_with(own_key, extent, deviation, reach, split, heavy, kind=jnp.bfloat16):
    array = deviation * jax.random.normal(own_key, extent, jnp.float32)
    if split:
        array = array * shard_levels(own_key, extent, split, -0.22, 0.18)
    return jnp.clip(spiked(array, jax.random.fold_in(own_key, 3), *heavy), -reach, reach).astype(kind)


def setup_inputs(seed: int = 0) -> dict:
    key_of = jax.random.split(jax.random.key(seed), 5)
    pair_grad = gaussian_with(key_of[0], (LEFT, RIGHT, PAIR), (ROWS // 64), 128.0, ((0, 8), (1, 4)), (1, 0, 8, 2.0))
    out_weight = scatter_about(key_of[1], (C * C, PAIR), (C * C) ** -0.5, 0.1875)
    left_feat = scatter_about(key_of[2], (LEFT, C, ROWS), 1.0, 6.0, ((0, 4), (2, 8)))
    right_feat = scatter_about(key_of[3], (RIGHT, C, ROWS), 1.0, 6.0, ((0, 4), (2, 8)))
    return {"pair_grad": pair_grad, "out_weight": out_weight, "left_feat": left_feat, "right_feat": right_feat}


def reference(pair_grad, out_weight, left_feat, right_feat):
    right_wide = right_feat.astype(jnp.float32)

    def panel(carry, index):
        first = (index * PANEL).astype(jnp.int32)
        grad_rows = lax.dynamic_slice_in_dim(pair_grad, first, PANEL, 0)
        flat = grad_rows.reshape(PANEL * RIGHT, PAIR)
        outer = lax.dot_general(flat, out_weight, (((1,), (1,)), ((), ())), preferred_element_type=jnp.float32)
        outer = outer.astype(jnp.bfloat16).reshape(PANEL, RIGHT, C, C).astype(jnp.float32)
        left_rows = lax.dynamic_slice_in_dim(left_feat, first, PANEL, 0).astype(jnp.float32)
        left_part = jnp.einsum("ijce,jes->ics", outer, right_wide)
        right_part = jnp.einsum("ijce,ics->jes", outer, left_rows)
        return carry + right_part, left_part

    start = jnp.zeros((RIGHT, C, ROWS), jnp.float32)
    right_total, left_parts = lax.scan(panel, start, jnp.arange(LEFT // PANEL, dtype=jnp.int32))
    grad_left = left_parts.reshape(LEFT, C, ROWS) / ROWS
    grad_right = right_total / ROWS
    return grad_left, grad_right
```

```python
import functools
import math

import jax
import jax.numpy as jnp
from jax import lax
from jax.experimental import pallas as pl
from jax.experimental.pallas import tpu as pltpu
from jax.sharding import PartitionSpec as P

MESH = pl.DeviceIdType.MESH
LANES = 128


def kernel(
    sizes, pair_in, weight_in, left_in, right_in, left_out, right_out,
    pair_all, left_all, sum_recv, sum_send, sum_own, raw, wide, right_perm,
    weight_raw, weight_wide, weight_perm, outer, right_acc, left_final,
    local_sem, pair_recv, pair_send, left_recv, left_send, sum_recv_sem, sum_send_sem, out_sem,
):
    n_seq, n_res, i_loc, n_right, width, rows = sizes
    chips = n_seq // 2
    chunk = 2 * i_loc
    n_left = n_seq * i_loc
    owned = n_left // n_res
    piece = math.gcd(chunk, owned)
    inverse = 1.0 / (rows * n_seq)
    q = lax.axis_index("seq")
    r = lax.axis_index("res")
    core = lax.rem(q, 2)
    chip = lax.div(q, 2)
    sibling = chip * 2 + (1 - core)
    lane_blocks = rows // LANES

    block = i_loc * n_right
    share = owned * width

    def pair_slot(source):
        return pair_all.at[pl.ds(pl.multiple_of(source * block, block), block), :]

    def left_slot(source):
        return left_all.at[pl.ds(pl.multiple_of(source * share, share), share), :]

    weight_copy = pltpu.make_async_copy(weight_in, weight_raw, local_sem.at[0])
    weight_copy.start()
    right_copy = pltpu.make_async_copy(right_in, raw, local_sem.at[1])
    right_copy.start()
    left_copy = pltpu.make_async_copy(left_in, left_slot(r), local_sem.at[2])
    left_copy.start()
    pair_copy = pltpu.make_async_copy(pair_in, pair_slot(q), local_sem.at[3])
    pair_copy.start()

    barrier = pltpu.get_barrier_semaphore()

    def greet(seq, res):
        pl.semaphore_signal(
            barrier, inc=1, device_id={"seq": seq, "res": res}, device_id_type=MESH
        )

    has_right = chip < chips - 1
    has_left = chip > 0

    @pl.when(has_right)
    def _():
        greet(q + 2, r)

    @pl.when(has_left)
    def _():
        greet(q - 2, r)

    greet(sibling, r)
    for step in range(1, n_res):
        greet(q, lax.rem(r + step, n_res))

    pl.semaphore_wait(
        barrier, n_res + has_right.astype(jnp.int32) + has_left.astype(jnp.int32)
    )

    def pair_send_to(source_ref, source, way, target):
        return pltpu.make_async_remote_copy(
            src_ref=source_ref, dst_ref=pair_slot(source),
            send_sem=pair_send.at[way, source], recv_sem=pair_recv.at[source],
            device_id={"seq": target, "res": r}, device_id_type=MESH,
        )

    @pl.when(has_right)
    def _():
        pair_send_to(pair_in, q, 0, q + 2).start()

    @pl.when(has_left)
    def _():
        pair_send_to(pair_in, q, 1, q - 2).start()

    pair_send_to(pair_in, q, 2, sibling).start()

    def left_send_to(step):
        return pltpu.make_async_remote_copy(
            src_ref=left_in, dst_ref=left_slot(r),
            send_sem=left_send.at[step], recv_sem=left_recv.at[r],
            device_id={"seq": q, "res": lax.rem(r + step, n_res)}, device_id_type=MESH,
        )

    for step in range(1, n_res):
        left_send_to(step).start()

    weight_copy.wait()
    weight_wide[...] = weight_raw[...].astype(jnp.float32)
    for e in range(width):
        weight_perm[e * width : (e + 1) * width, :] = weight_wide[
            pl.ds(e, width, stride=width), :
        ].astype(jnp.bfloat16)
    right_copy.wait()
    for b in range(lane_blocks):
        lanes = slice(b * LANES, (b + 1) * LANES)
        wide[b] = raw[:, lanes].astype(jnp.float32)
        for e in range(width):
            right_perm[e * n_right : (e + 1) * n_right, lanes] = wide[
                b, pl.ds(e, n_right, stride=width), :
            ].astype(jnp.bfloat16)
    right_acc[...] = jnp.zeros_like(right_acc)

    left_copy.wait()
    pair_copy.wait()
    for step in range(1, n_res):
        source = lax.rem(r + step, n_res)
        pltpu.make_async_copy(left_slot(source), left_slot(source), left_recv.at[source]).wait()

    def pair_wait(source):
        pltpu.make_async_copy(pair_slot(source), pair_slot(source), pair_recv.at[source]).wait()

    def sum_send_to(index, owner):
        offset = lax.rem(index * piece, owned) * width
        return pltpu.make_async_remote_copy(
            src_ref=sum_send.at[pl.ds(pl.multiple_of(index * piece * width, piece * width), piece * width), :],
            dst_ref=sum_recv.at[r, pl.ds(pl.multiple_of(offset, piece * width), piece * width), :],
            send_sem=sum_send_sem.at[index], recv_sem=sum_recv_sem.at[r],
            device_id={"seq": q, "res": owner}, device_id_type=MESH,
        )

    pieces = chunk // piece
    group = max(1, 256 // n_right)
    group = math.gcd(group, chunk)
    span = group * n_right
    columns = width * n_right
    tile = math.gcd(columns, 512)

    def compute(which):
        for p in range(chunk // group):
            start = pl.multiple_of(which * (chunk * n_right) + p * span, span)
            grads = pair_all[pl.ds(start, span), :]
            expanded = lax.dot_general(
                weight_perm[...], grads, (((1,), (1,)), ((), ())), preferred_element_type=jnp.float32
            ).astype(jnp.bfloat16)
            for ii in range(group):
                i = p * group + ii
                for e in range(width):
                    outer[i * width : (i + 1) * width, e * n_right : (e + 1) * n_right] = expanded[
                        e * width : (e + 1) * width, ii * n_right : (ii + 1) * n_right
                    ]
        part = lax.dot_general(
            outer[...], right_perm[...], (((1,), (0,)), ((), ())), preferred_element_type=jnp.float32
        ) * inverse
        first = pl.multiple_of(which * (chunk * width), chunk * width)
        sum_send[pl.ds(first, chunk * width), :] = part.astype(jnp.bfloat16)
        for u in range(pieces):
            index = which * pieces + u
            owner = lax.div(index * piece, owned)

            @pl.when(owner == r)
            def _():
                offset = pl.multiple_of(lax.rem(index * piece, owned) * width, piece * width)
                sum_own[pl.ds(offset, piece * width), :] = part[
                    u * piece * width : (u + 1) * piece * width, :
                ]

            @pl.when(owner != r)
            def _():
                sum_send_to(index, owner).start()

        left_rows = left_all[pl.ds(first, chunk * width), :]
        for t in range(columns // tile):
            at = slice(t * tile, (t + 1) * tile)
            right_acc[:, at] += lax.dot_general(
                left_rows, outer[:, at], (((0,), (0,)), ((), ())), preferred_element_type=jnp.float32
            )

    def ring(d, carry):
        lower = chip - d
        upper = chip + d

        @pl.when((d > 0) & (lower >= 0))
        def _():
            source = lower * 2 + core
            pair_wait(source)

            @pl.when(has_right)
            def _():
                pair_send_to(pair_slot(source), source, 0, q + 2).start()

            pair_send_to(pair_slot(source), source, 2, sibling).start()

        @pl.when((d > 0) & (upper < chips))
        def _():
            source = upper * 2 + core
            pair_wait(source)

            @pl.when(has_left)
            def _():
                pair_send_to(pair_slot(source), source, 1, q - 2).start()

            pair_send_to(pair_slot(source), source, 2, sibling).start()

        def side(s, inner):
            which = chip + (2 * s - 1) * d

            @pl.when((which >= 0) & (which < chips) & ((d > 0) | (s == 0)))
            def _():
                pair_wait(which * 2 + (1 - core))
                compute(which)

            return inner

        return lax.fori_loop(0, 2, side, carry)

    lax.fori_loop(0, chips, ring, 0)

    for b in range(lane_blocks):
        lanes = slice(b * LANES, (b + 1) * LANES)
        for e in range(width):
            wide[b, pl.ds(e, n_right, stride=width), :] = (
                jnp.transpose(right_acc[lanes, e * n_right : (e + 1) * n_right]) * inverse
            )
    right_copies = [
        pltpu.make_async_copy(
            wide.at[b], right_out.at[:, pl.ds(b * LANES, LANES)], out_sem.at[b]
        )
        for b in range(lane_blocks)
    ]
    for copy in right_copies:
        copy.start()

    total = sum_own[...]
    for step in range(1, n_res):
        source = lax.rem(r + step, n_res)
        pltpu.make_async_copy(sum_recv.at[source], sum_recv.at[source], sum_recv_sem.at[source]).wait()
        total = total + sum_recv[source].astype(jnp.float32)
    left_final[...] = total
    final_copy = pltpu.make_async_copy(left_final, left_out, out_sem.at[lane_blocks])
    final_copy.start()

    pair_send_to(pair_in, q, 2, sibling).wait_send()

    @pl.when(has_right)
    def _():
        pair_send_to(pair_in, q, 0, q + 2).wait_send()

    @pl.when(has_left)
    def _():
        pair_send_to(pair_in, q, 1, q - 2).wait_send()

    def settle(d, carry):
        lower = chip - d
        upper = chip + d

        @pl.when(lower >= 0)
        def _():
            source = lower * 2 + core

            @pl.when(has_right)
            def _():
                pair_send_to(pair_slot(source), source, 0, q + 2).wait_send()

            pair_send_to(pair_slot(source), source, 2, sibling).wait_send()

        @pl.when(upper < chips)
        def _():
            source = upper * 2 + core

            @pl.when(has_left)
            def _():
                pair_send_to(pair_slot(source), source, 1, q - 2).wait_send()

            pair_send_to(pair_slot(source), source, 2, sibling).wait_send()

        return carry

    lax.fori_loop(1, chips, settle, 0)
    for step in range(1, n_res):
        left_send_to(step).wait_send()

    def settle_sums(index, carry):
        owner = lax.div(index * piece, owned)

        @pl.when(owner != r)
        def _():
            sum_send_to(index, owner).wait_send()

        return carry

    lax.fori_loop(0, n_left // piece, settle_sums, 0)
    final_copy.wait()
    for copy in right_copies:
        copy.wait()


def per_device(n_seq, n_res, pair_grad, out_weight, left_feat, right_feat):
    i_loc, n_right, pair = pair_grad.shape
    owned, width, rows = left_feat.shape
    n_left = n_seq * i_loc
    chunk = 2 * i_loc
    piece = math.gcd(chunk, owned)
    sizes = (n_seq, n_res, i_loc, n_right, width, rows)
    lane_blocks = rows // LANES
    bf16, f32 = jnp.bfloat16, jnp.float32
    dma = pltpu.SemaphoreType.DMA
    anywhere = pl.BlockSpec(memory_space=pl.ANY)
    grad_left, grad_right = pl.pallas_call(
        functools.partial(kernel, sizes),
        out_shape=(
            jax.ShapeDtypeStruct((owned * width, rows), f32),
            jax.ShapeDtypeStruct((n_right * width, rows), f32),
        ),
        in_specs=[anywhere] * 4,
        out_specs=(anywhere, anywhere),
        scratch_shapes=[
            pltpu.VMEM((n_left * n_right, pair), bf16),
            pltpu.VMEM((n_left * width, rows), bf16),
            pltpu.VMEM((n_res, owned * width, rows), bf16),
            pltpu.VMEM((n_left * width, rows), bf16),
            pltpu.VMEM((owned * width, rows), f32),
            pltpu.VMEM((n_right * width, rows), bf16),
            pltpu.VMEM((lane_blocks, n_right * width, LANES), f32),
            pltpu.VMEM((width * n_right, rows), bf16),
            pltpu.VMEM((width * width, pair), bf16),
            pltpu.VMEM((width * width, pair), f32),
            pltpu.VMEM((width * width, pair), bf16),
            pltpu.VMEM((chunk * width, width * n_right), bf16),
            pltpu.VMEM((rows, width * n_right), f32),
            pltpu.VMEM((owned * width, rows), f32),
            dma((4,)),
            dma((n_seq,)),
            dma((3, n_seq)),
            dma((n_res,)),
            dma((n_res,)),
            dma((n_res,)),
            dma((n_left // piece,)),
            dma((lane_blocks + 1,)),
        ],
        compiler_params=pltpu.CompilerParams(
            collective_id=0, has_side_effects=True, vmem_limit_bytes=48 * 1024 * 1024
        ),
    )(
        pair_grad.reshape(i_loc * n_right, pair),
        out_weight,
        left_feat.reshape(owned * width, rows),
        right_feat.reshape(n_right * width, rows),
    )
    return (
        grad_left.reshape(owned, width, rows),
        grad_right.reshape(n_right, width, rows),
    )


def solution(mesh):
    in_specs = (P("seq", "res", None), P(), P("res", None, "seq"), P("res", None, "seq"))
    out_specs = (P("res", None, "seq"), P("res", None, "seq"))
    body = functools.partial(per_device, mesh.shape["seq"], mesh.shape["res"])
    return jax.shard_map(body, mesh=mesh, in_specs=in_specs, out_specs=out_specs, check_vma=False)
```

```python
import functools
import math

import jax
import jax.numpy as jnp
from jax import lax
from jax.experimental import pallas as pl
from jax.experimental.pallas import tpu as pltpu
from jax.sharding import PartitionSpec as P

MESH = pl.DeviceIdType.MESH
LANES = 128


def kernel(
    sizes, pair_in, weight_in, left_in, right_in, left_out, right_out,
    pair_all, left_all, sum_recv, sum_send, sum_own, raw, wide, right_perm,
    weight_raw, weight_wide, weight_perm, outer, right_acc,
    local_sem, pair_recv, pair_send, left_recv, left_send, sum_recv_sem, sum_send_sem,
):
    n_seq, n_res, i_loc, n_right, width, rows = sizes
    chips = n_seq // 2
    chunk = 2 * i_loc
    n_left = n_seq * i_loc
    owned = n_left // n_res
    piece = math.gcd(chunk, owned)
    inverse = 1.0 / (rows * n_seq)
    q = lax.axis_index("seq")
    r = lax.axis_index("res")
    core = lax.rem(q, 2)
    chip = lax.div(q, 2)
    sibling = chip * 2 + (1 - core)
    lane_blocks = rows // LANES

    block = i_loc * n_right
    share = owned * width

    def pair_slot(source):
        return pair_all.at[pl.ds(pl.multiple_of(source * block, block), block), :]

    def left_slot(source):
        return left_all.at[pl.ds(pl.multiple_of(source * share, share), share), :]

    weight_copy = pltpu.make_async_copy(weight_in, weight_raw, local_sem.at[0])
    weight_copy.start()
    right_copy = pltpu.make_async_copy(right_in, raw, local_sem.at[1])
    right_copy.start()
    left_copy = pltpu.make_async_copy(left_in, left_slot(r), local_sem.at[2])
    left_copy.start()
    pair_copy = pltpu.make_async_copy(pair_in, pair_slot(q), local_sem.at[3])
    pair_copy.start()

    barrier = pltpu.get_barrier_semaphore()

    def greet(seq, res):
        pl.semaphore_signal(
            barrier, inc=1, device_id={"seq": seq, "res": res}, device_id_type=MESH
        )

    has_right = chip < chips - 1
    has_left = chip > 0

    @pl.when(has_right)
    def _():
        greet(q + 2, r)

    @pl.when(has_left)
    def _():
        greet(q - 2, r)

    greet(sibling, r)
    for step in range(1, n_res):
        greet(q, lax.rem(r + step, n_res))

    pl.semaphore_wait(
        barrier, n_res + has_right.astype(jnp.int32) + has_left.astype(jnp.int32)
    )

    def pair_send_to(source_ref, source, way, target):
        return pltpu.make_async_remote_copy(
            src_ref=source_ref, dst_ref=pair_slot(source),
            send_sem=pair_send.at[way, source], recv_sem=pair_recv.at[source],
            device_id={"seq": target, "res": r}, device_id_type=MESH,
        )

    @pl.when(has_right)
    def _():
        pair_send_to(pair_in, q, 0, q + 2).start()

    @pl.when(has_left)
    def _():
        pair_send_to(pair_in, q, 1, q - 2).start()

    pair_send_to(pair_in, q, 2, sibling).start()

    def left_send_to(step):
        return pltpu.make_async_remote_copy(
            src_ref=left_in, dst_ref=left_slot(r),
            send_sem=left_send.at[step], recv_sem=left_recv.at[r],
            device_id={"seq": q, "res": lax.rem(r + step, n_res)}, device_id_type=MESH,
        )

    for step in range(1, n_res):
        left_send_to(step).start()

    weight_copy.wait()
    weight_wide[...] = weight_raw[...].astype(jnp.float32)
    for e in range(width):
        weight_perm[e * width : (e + 1) * width, :] = weight_wide[
            pl.ds(e, width, stride=width), :
        ].astype(jnp.bfloat16)
    right_copy.wait()
    for b in range(lane_blocks):
        lanes = slice(b * LANES, (b + 1) * LANES)
        wide[b] = raw[:, lanes].astype(jnp.float32)
        for e in range(width):
            right_perm[e * n_right : (e + 1) * n_right, lanes] = wide[
                b, pl.ds(e, n_right, stride=width), :
            ].astype(jnp.bfloat16)
    right_acc[...] = jnp.zeros_like(right_acc)

    left_copy.wait()
    pair_copy.wait()
    for step in range(1, n_res):
        source = lax.rem(r + step, n_res)
        pltpu.make_async_copy(left_slot(source), left_slot(source), left_recv.at[source]).wait()

    def pair_wait(source):
        pltpu.make_async_copy(pair_slot(source), pair_slot(source), pair_recv.at[source]).wait()

    def sum_send_to(index, owner):
        offset = lax.rem(index * piece, owned) * width
        return pltpu.make_async_remote_copy(
            src_ref=sum_send.at[pl.ds(pl.multiple_of(index * piece * width, piece * width), piece * width), :],
            dst_ref=sum_recv.at[r, pl.ds(pl.multiple_of(offset, piece * width), piece * width), :],
            send_sem=sum_send_sem.at[index], recv_sem=sum_recv_sem.at[r],
            device_id={"seq": q, "res": owner}, device_id_type=MESH,
        )

    pieces = chunk // piece
    group = max(1, 256 // n_right)
    group = math.gcd(group, chunk)
    span = group * n_right
    columns = width * n_right
    tile = math.gcd(columns, 512)

    def compute(which):
        for p in range(chunk // group):
            start = pl.multiple_of(which * (chunk * n_right) + p * span, span)
            grads = pair_all[pl.ds(start, span), :]
            expanded = lax.dot_general(
                weight_perm[...], grads, (((1,), (1,)), ((), ())), preferred_element_type=jnp.float32
            ).astype(jnp.bfloat16)
            for ii in range(group):
                i = p * group + ii
                for e in range(width):
                    outer[i * width : (i + 1) * width, e * n_right : (e + 1) * n_right] = expanded[
                        e * width : (e + 1) * width, ii * n_right : (ii + 1) * n_right
                    ]
        part = lax.dot_general(
            outer[...], right_perm[...], (((1,), (0,)), ((), ())), preferred_element_type=jnp.float32
        ) * inverse
        first = pl.multiple_of(which * (chunk * width), chunk * width)
        sum_send[pl.ds(first, chunk * width), :] = part.astype(jnp.bfloat16)
        for u in range(pieces):
            index = which * pieces + u
            owner = lax.div(index * piece, owned)

            @pl.when(owner == r)
            def _():
                offset = pl.multiple_of(lax.rem(index * piece, owned) * width, piece * width)
                sum_own[pl.ds(offset, piece * width), :] = part[
                    u * piece * width : (u + 1) * piece * width, :
                ]

            @pl.when(owner != r)
            def _():
                sum_send_to(index, owner).start()

        left_rows = left_all[pl.ds(first, chunk * width), :]
        for t in range(columns // tile):
            at = slice(t * tile, (t + 1) * tile)
            right_acc[:, at] += lax.dot_general(
                left_rows, outer[:, at], (((0,), (0,)), ((), ())), preferred_element_type=jnp.float32
            )

    def ring(d, carry):
        lower = chip - d
        upper = chip + d

        @pl.when((d > 0) & (lower >= 0))
        def _():
            source = lower * 2 + core
            pair_wait(source)

            @pl.when(has_right)
            def _():
                pair_send_to(pair_slot(source), source, 0, q + 2).start()

            pair_send_to(pair_slot(source), source, 2, sibling).start()

        @pl.when((d > 0) & (upper < chips))
        def _():
            source = upper * 2 + core
            pair_wait(source)

            @pl.when(has_left)
            def _():
                pair_send_to(pair_slot(source), source, 1, q - 2).start()

            pair_send_to(pair_slot(source), source, 2, sibling).start()

        def side(s, inner):
            which = chip + (2 * s - 1) * d

            @pl.when((which >= 0) & (which < chips) & ((d > 0) | (s == 0)))
            def _():
                pair_wait(which * 2 + (1 - core))
                compute(which)

            return inner

        return lax.fori_loop(0, 2, side, carry)

    lax.fori_loop(0, chips, ring, 0)

    for b in range(lane_blocks):
        lanes = slice(b * LANES, (b + 1) * LANES)
        for e in range(width):
            right_out[b, pl.ds(e, n_right, stride=width), :] = (
                jnp.transpose(right_acc[lanes, e * n_right : (e + 1) * n_right]) * inverse
            )
    total = sum_own[...]
    for step in range(1, n_res):
        source = lax.rem(r + step, n_res)
        pltpu.make_async_copy(sum_recv.at[source], sum_recv.at[source], sum_recv_sem.at[source]).wait()
        total = total + sum_recv[source].astype(jnp.float32)
    left_out[...] = total

    pair_send_to(pair_in, q, 2, sibling).wait_send()

    @pl.when(has_right)
    def _():
        pair_send_to(pair_in, q, 0, q + 2).wait_send()

    @pl.when(has_left)
    def _():
        pair_send_to(pair_in, q, 1, q - 2).wait_send()

    def settle(d, carry):
        lower = chip - d
        upper = chip + d

        @pl.when(lower >= 0)
        def _():
            source = lower * 2 + core

            @pl.when(has_right)
            def _():
                pair_send_to(pair_slot(source), source, 0, q + 2).wait_send()

            pair_send_to(pair_slot(source), source, 2, sibling).wait_send()

        @pl.when(upper < chips)
        def _():
            source = upper * 2 + core

            @pl.when(has_left)
            def _():
                pair_send_to(pair_slot(source), source, 1, q - 2).wait_send()

            pair_send_to(pair_slot(source), source, 2, sibling).wait_send()

        return carry

    lax.fori_loop(1, chips, settle, 0)
    for step in range(1, n_res):
        left_send_to(step).wait_send()

    def settle_sums(index, carry):
        owner = lax.div(index * piece, owned)

        @pl.when(owner != r)
        def _():
            sum_send_to(index, owner).wait_send()

        return carry

    lax.fori_loop(0, n_left // piece, settle_sums, 0)


def per_device(n_seq, n_res, pair_grad, out_weight, left_feat, right_feat):
    i_loc, n_right, pair = pair_grad.shape
    owned, width, rows = left_feat.shape
    n_left = n_seq * i_loc
    chunk = 2 * i_loc
    piece = math.gcd(chunk, owned)
    sizes = (n_seq, n_res, i_loc, n_right, width, rows)
    lane_blocks = rows // LANES
    bf16, f32 = jnp.bfloat16, jnp.float32
    dma = pltpu.SemaphoreType.DMA
    grad_left, grad_right = pl.pallas_call(
        functools.partial(kernel, sizes),
        out_shape=(
            jax.ShapeDtypeStruct((owned * width, rows), f32),
            jax.ShapeDtypeStruct((lane_blocks, n_right * width, LANES), f32),
        ),
        in_specs=[pl.BlockSpec(memory_space=pltpu.HBM)] * 4,
        out_specs=(pl.BlockSpec(memory_space=pltpu.VMEM),) * 2,
        scratch_shapes=[
            pltpu.VMEM((n_left * n_right, pair), bf16),
            pltpu.VMEM((n_left * width, rows), bf16),
            pltpu.VMEM((n_res, owned * width, rows), bf16),
            pltpu.VMEM((n_left * width, rows), bf16),
            pltpu.VMEM((owned * width, rows), f32),
            pltpu.VMEM((n_right * width, rows), bf16),
            pltpu.VMEM((lane_blocks, n_right * width, LANES), f32),
            pltpu.VMEM((width * n_right, rows), bf16),
            pltpu.VMEM((width * width, pair), bf16),
            pltpu.VMEM((width * width, pair), f32),
            pltpu.VMEM((width * width, pair), bf16),
            pltpu.VMEM((chunk * width, width * n_right), bf16),
            pltpu.VMEM((rows, width * n_right), f32),
            dma((4,)),
            dma((n_seq,)),
            dma((3, n_seq)),
            dma((n_res,)),
            dma((n_res,)),
            dma((n_res,)),
            dma((n_left // piece,)),
        ],
        compiler_params=pltpu.CompilerParams(
            collective_id=0, has_side_effects=True, vmem_limit_bytes=48 * 1024 * 1024
        ),
    )(
        *(
            pltpu.with_memory_space_constraint(x, pltpu.HBM)
            for x in (
                pair_grad.reshape(i_loc * n_right, pair),
                out_weight,
                left_feat.reshape(owned * width, rows),
                right_feat.reshape(n_right * width, rows),
            )
        )
    )
    return (
        grad_left.reshape(owned, width, rows),
        jnp.moveaxis(grad_right, 0, 1).reshape(n_right, width, rows),
    )


def solution(mesh):
    in_specs = (P("seq", "res", None), P(), P("res", None, "seq"), P("res", None, "seq"))
    out_specs = (P("res", None, "seq"), P("res", None, "seq"))
    body = functools.partial(per_device, mesh.shape["seq"], mesh.shape["res"])
    return jax.shard_map(body, mesh=mesh, in_specs=in_specs, out_specs=out_specs, check_vma=False)
```

```python
import functools
import math

import jax
import jax.numpy as jnp
from jax import lax
from jax.experimental import pallas as pl
from jax.experimental.pallas import tpu as pltpu
from jax.sharding import PartitionSpec as P

MESH = pl.DeviceIdType.MESH
LANES = 128


def kernel(
    sizes, pair_in, weight_in, left_in, right_in, left_out, right_out,
    pair_all, left_all, sum_recv, sum_send, sum_own, raw, wide, right_perm,
    weight_raw, weight_wide, weight_perm, outer, right_acc,
    local_sem, pair_recv, pair_send, left_recv, left_send, sum_recv_sem, sum_send_sem,
):
    n_seq, n_res, i_loc, n_right, width, rows = sizes
    chips = n_seq // 2
    chunk = 2 * i_loc
    n_left = n_seq * i_loc
    owned = n_left // n_res
    piece = math.gcd(chunk, owned)
    inverse = 1.0 / (rows * n_seq)
    q = lax.axis_index("seq")
    r = lax.axis_index("res")
    core = lax.rem(q, 2)
    chip = lax.div(q, 2)
    sibling = chip * 2 + (1 - core)
    lane_blocks = rows // LANES

    block = i_loc * n_right
    share = owned * width

    def pair_slot(source):
        return pair_all.at[pl.ds(pl.multiple_of(source * block, block), block), :]

    def left_slot(source):
        return left_all.at[pl.ds(pl.multiple_of(source * share, share), share), :]

    weight_copy = pltpu.make_async_copy(weight_in, weight_raw, local_sem.at[0])
    weight_copy.start()
    right_copy = pltpu.make_async_copy(right_in, raw, local_sem.at[1])
    right_copy.start()
    left_copy = pltpu.make_async_copy(left_in, left_slot(r), local_sem.at[2])
    left_copy.start()
    pair_copy = pltpu.make_async_copy(pair_in, pair_slot(q), local_sem.at[3])
    pair_copy.start()

    barrier = pltpu.get_barrier_semaphore()

    def greet(seq, res):
        pl.semaphore_signal(
            barrier, inc=1, device_id={"seq": seq, "res": res}, device_id_type=MESH
        )

    has_right = chip < chips - 1
    has_left = chip > 0

    @pl.when(has_right)
    def _():
        greet(q + 2, r)

    @pl.when(has_left)
    def _():
        greet(q - 2, r)

    greet(sibling, r)
    for step in range(1, n_res):
        greet(q, lax.rem(r + step, n_res))

    pl.semaphore_wait(
        barrier, n_res + has_right.astype(jnp.int32) + has_left.astype(jnp.int32)
    )

    def pair_piece(source, p):
        start = source * block + p * n_right
        return pair_all.at[pl.ds(pl.multiple_of(start, n_right), n_right), :]

    def pair_send_to(source_ref, source, p, way, target):
        return pltpu.make_async_remote_copy(
            src_ref=source_ref, dst_ref=pair_piece(source, p),
            send_sem=pair_send.at[way, source, p], recv_sem=pair_recv.at[source, p],
            device_id={"seq": target, "res": r}, device_id_type=MESH,
        )

    def own_sends(act):
        for p in range(i_loc):
            own = pair_in.at[pl.ds(p * n_right, n_right), :]

            @pl.when(has_right)
            def _():
                act(pair_send_to(own, q, p, 0, q + 2))

            @pl.when(has_left)
            def _():
                act(pair_send_to(own, q, p, 1, q - 2))

            act(pair_send_to(own, q, p, 2, sibling))

    def relay(d, p, first, act):
        lower = chip - d
        upper = chip + d

        @pl.when(lower >= 0)
        def _():
            source = lower * 2 + core
            first(source, p)

            @pl.when(has_right)
            def _():
                act(pair_send_to(pair_piece(source, p), source, p, 0, q + 2))

            act(pair_send_to(pair_piece(source, p), source, p, 2, sibling))

        @pl.when(upper < chips)
        def _():
            source = upper * 2 + core
            first(source, p)

            @pl.when(has_left)
            def _():
                act(pair_send_to(pair_piece(source, p), source, p, 1, q - 2))

            act(pair_send_to(pair_piece(source, p), source, p, 2, sibling))

    own_sends(lambda copy: copy.start())

    def left_send_to(step):
        return pltpu.make_async_remote_copy(
            src_ref=left_in, dst_ref=left_slot(r),
            send_sem=left_send.at[step], recv_sem=left_recv.at[r],
            device_id={"seq": q, "res": lax.rem(r + step, n_res)}, device_id_type=MESH,
        )

    for step in range(1, n_res):
        left_send_to(step).start()

    weight_copy.wait()
    weight_wide[...] = weight_raw[...].astype(jnp.float32)
    for e in range(width):
        weight_perm[e * width : (e + 1) * width, :] = weight_wide[
            pl.ds(e, width, stride=width), :
        ].astype(jnp.bfloat16)
    right_copy.wait()
    for b in range(lane_blocks):
        lanes = slice(b * LANES, (b + 1) * LANES)
        wide[b] = raw[:, lanes].astype(jnp.float32)
        for e in range(width):
            right_perm[e * n_right : (e + 1) * n_right, lanes] = wide[
                b, pl.ds(e, n_right, stride=width), :
            ].astype(jnp.bfloat16)
    right_acc[...] = jnp.zeros_like(right_acc)

    pair_copy.wait()

    def left_wait():
        left_copy.wait()
        for step in range(1, n_res):
            source = lax.rem(r + step, n_res)
            pltpu.make_async_copy(left_slot(source), left_slot(source), left_recv.at[source]).wait()

    def pair_wait(source, p):
        pltpu.make_async_copy(
            pair_piece(source, p), pair_piece(source, p), pair_recv.at[source, p]
        ).wait()

    def sum_send_to(index, owner):
        offset = lax.rem(index * piece, owned) * width
        return pltpu.make_async_remote_copy(
            src_ref=sum_send.at[pl.ds(pl.multiple_of(index * piece * width, piece * width), piece * width), :],
            dst_ref=sum_recv.at[r, pl.ds(pl.multiple_of(offset, piece * width), piece * width), :],
            send_sem=sum_send_sem.at[index], recv_sem=sum_recv_sem.at[r],
            device_id={"seq": q, "res": owner}, device_id_type=MESH,
        )

    pieces = chunk // piece
    group = max(1, 256 // n_right)
    group = math.gcd(group, chunk)
    span = group * n_right
    columns = width * n_right
    tile = math.gcd(columns, 512)

    halves = chunk // group

    def expand(which, s, low, high):
        for p in range(low, high):
            start = pl.multiple_of(which * (chunk * n_right) + p * span, span)
            grads = pair_all[pl.ds(start, span), :]
            expanded = lax.dot_general(
                weight_perm[...], grads, (((1,), (1,)), ((), ())), preferred_element_type=jnp.float32
            ).astype(jnp.bfloat16)
            for ii in range(group):
                i = p * group + ii
                for e in range(width):
                    outer[s, i * width : (i + 1) * width, e * n_right : (e + 1) * n_right] = expanded[
                        e * width : (e + 1) * width, ii * n_right : (ii + 1) * n_right
                    ]

    def stage_wait(which, s):
        for p in range(i_loc):
            pair_wait(which * 2 + (1 - core), p)
        expand(which, s, 0, halves // 2)

    def stage_expand(which, s):
        expand(which, s, halves // 2, halves)

    def stage_left(which, s):
        part = lax.dot_general(
            outer[s], right_perm[...], (((1,), (0,)), ((), ())), preferred_element_type=jnp.float32
        ) * inverse
        first = pl.multiple_of(which * (chunk * width), chunk * width)
        sum_send[pl.ds(first, chunk * width), :] = part.astype(jnp.bfloat16)
        for u in range(pieces):
            index = which * pieces + u
            owner = lax.div(index * piece, owned)

            @pl.when(owner == r)
            def _():
                offset = pl.multiple_of(lax.rem(index * piece, owned) * width, piece * width)
                sum_own[pl.ds(offset, piece * width), :] = part[
                    u * piece * width : (u + 1) * piece * width, :
                ]

            @pl.when(owner != r)
            def _():
                sum_send_to(index, owner).start()

    def stage_right(which, s):
        first = pl.multiple_of(which * (chunk * width), chunk * width)
        left_rows = left_all[pl.ds(first, chunk * width), :]
        for t in range(columns // tile):
            at = slice(t * tile, (t + 1) * tile)
            right_acc[:, at] += lax.dot_general(
                left_rows, outer[s, :, at], (((0,), (0,)), ((), ())), preferred_element_type=jnp.float32
            )

    stages = [stage_wait, stage_expand, stage_left, stage_right]

    def ring(d, carry):
        for p in range(i_loc):
            relay(d, p, pair_wait, lambda copy: copy.start())
            if p == i_loc - 1:
                pl.when(d == 1)(left_wait)
            todo = stages[p * len(stages) // i_loc : (p + 1) * len(stages) // i_loc]

            def side(s, inner):
                which = chip + (2 * s - 1) * (d - 1)

                @pl.when((which >= 0) & (which < chips) & ((d > 1) | (s == 0)))
                def _():
                    for stage in todo:
                        stage(which, s)

                return inner

            lax.fori_loop(0, 2, side, 0)
        return carry

    lax.fori_loop(1, chips + 1, ring, 0)

    for b in range(lane_blocks):
        lanes = slice(b * LANES, (b + 1) * LANES)
        for e in range(width):
            right_out[b, pl.ds(e, n_right, stride=width), :] = (
                jnp.transpose(right_acc[lanes, e * n_right : (e + 1) * n_right]) * inverse
            )
    total = sum_own[...]
    for step in range(1, n_res):
        source = lax.rem(r + step, n_res)
        pltpu.make_async_copy(sum_recv.at[source], sum_recv.at[source], sum_recv_sem.at[source]).wait()
        total = total + sum_recv[source].astype(jnp.float32)
    left_out[...] = total

    own_sends(lambda copy: copy.wait_send())

    def settle(d, carry):
        for p in range(i_loc):
            relay(d, p, lambda source, p: None, lambda copy: copy.wait_send())
        return carry

    lax.fori_loop(1, chips, settle, 0)
    for step in range(1, n_res):
        left_send_to(step).wait_send()

    def settle_sums(index, carry):
        owner = lax.div(index * piece, owned)

        @pl.when(owner != r)
        def _():
            sum_send_to(index, owner).wait_send()

        return carry

    lax.fori_loop(0, n_left // piece, settle_sums, 0)


def per_device(n_seq, n_res, pair_grad, out_weight, left_feat, right_feat):
    i_loc, n_right, pair = pair_grad.shape
    owned, width, rows = left_feat.shape
    n_left = n_seq * i_loc
    chunk = 2 * i_loc
    piece = math.gcd(chunk, owned)
    sizes = (n_seq, n_res, i_loc, n_right, width, rows)
    lane_blocks = rows // LANES
    bf16, f32 = jnp.bfloat16, jnp.float32
    dma = pltpu.SemaphoreType.DMA
    grad_left, grad_right = pl.pallas_call(
        functools.partial(kernel, sizes),
        out_shape=(
            jax.ShapeDtypeStruct((owned * width, rows), f32),
            jax.ShapeDtypeStruct((lane_blocks, n_right * width, LANES), f32),
        ),
        in_specs=[pl.BlockSpec(memory_space=pltpu.HBM)] * 4,
        out_specs=(pl.BlockSpec(memory_space=pltpu.VMEM),) * 2,
        scratch_shapes=[
            pltpu.VMEM((n_left * n_right, pair), bf16),
            pltpu.VMEM((n_left * width, rows), bf16),
            pltpu.VMEM((n_res, owned * width, rows), bf16),
            pltpu.VMEM((n_left * width, rows), bf16),
            pltpu.VMEM((owned * width, rows), f32),
            pltpu.VMEM((n_right * width, rows), bf16),
            pltpu.VMEM((lane_blocks, n_right * width, LANES), f32),
            pltpu.VMEM((width * n_right, rows), bf16),
            pltpu.VMEM((width * width, pair), bf16),
            pltpu.VMEM((width * width, pair), f32),
            pltpu.VMEM((width * width, pair), bf16),
            pltpu.VMEM((2, chunk * width, width * n_right), bf16),
            pltpu.VMEM((rows, width * n_right), f32),
            dma((4,)),
            dma((n_seq, i_loc)),
            dma((3, n_seq, i_loc)),
            dma((n_res,)),
            dma((n_res,)),
            dma((n_res,)),
            dma((n_left // piece,)),
        ],
        compiler_params=pltpu.CompilerParams(
            collective_id=0, has_side_effects=True, vmem_limit_bytes=48 * 1024 * 1024
        ),
    )(
        *(
            pltpu.with_memory_space_constraint(x, pltpu.HBM)
            for x in (
                pair_grad.reshape(i_loc * n_right, pair),
                out_weight,
                left_feat.reshape(owned * width, rows),
                right_feat.reshape(n_right * width, rows),
            )
        )
    )
    return (
        grad_left.reshape(owned, width, rows),
        jnp.moveaxis(grad_right, 0, 1).reshape(n_right, width, rows),
    )


def solution(mesh):
    in_specs = (P("seq", "res", None), P(), P("res", None, "seq"), P("res", None, "seq"))
    out_specs = (P("res", None, "seq"), P("res", None, "seq"))
    body = functools.partial(per_device, mesh.shape["seq"], mesh.shape["res"])
    return jax.shard_map(body, mesh=mesh, in_specs=in_specs, out_specs=out_specs, check_vma=False)
```

```python
import functools
import math

import jax
import jax.numpy as jnp
from jax import lax
from jax.experimental import pallas as pl
from jax.experimental.pallas import tpu as pltpu
from jax.sharding import PartitionSpec as P

MESH = pl.DeviceIdType.MESH
LANES = 128
PARTS = 2


def kernel(
    sizes, pair_in, weight_in, left_in, right_in, left_out, right_out,
    pair_all, left_all, sum_recv, sum_send, sum_own, raw, wide, right_perm,
    weight_raw, weight_wide, weight_perm, outer, right_acc,
    local_sem, pair_recv, pair_send, left_recv, left_send, sum_recv_sem, sum_send_sem,
):
    n_seq, n_res, i_loc, n_right, width, rows = sizes
    chips = n_seq // 2
    parts = math.gcd(i_loc, PARTS)
    chunk = 2 * i_loc
    n_left = n_seq * i_loc
    owned = n_left // n_res
    piece = math.gcd(chunk, owned)
    inverse = 1.0 / (rows * n_seq)
    q = lax.axis_index("seq")
    r = lax.axis_index("res")
    core = lax.rem(q, 2)
    chip = lax.div(q, 2)
    sibling = chip * 2 + (1 - core)
    lane_blocks = rows // LANES

    block = i_loc * n_right
    share = owned * width

    def pair_slot(source):
        return pair_all.at[pl.ds(pl.multiple_of(source * block, block), block), :]

    def left_slot(source):
        return left_all.at[pl.ds(pl.multiple_of(source * share, share), share), :]

    weight_copy = pltpu.make_async_copy(weight_in, weight_raw, local_sem.at[0])
    weight_copy.start()
    right_copy = pltpu.make_async_copy(right_in, raw, local_sem.at[1])
    right_copy.start()
    left_copy = pltpu.make_async_copy(left_in, left_slot(r), local_sem.at[2])
    left_copy.start()
    pair_copy = pltpu.make_async_copy(pair_in, pair_slot(q), local_sem.at[3])
    pair_copy.start()

    barrier = pltpu.get_barrier_semaphore()

    def greet(seq, res):
        pl.semaphore_signal(
            barrier, inc=1, device_id={"seq": seq, "res": res}, device_id_type=MESH
        )

    has_right = chip < chips - 1
    has_left = chip > 0

    @pl.when(has_right)
    def _():
        greet(q + 2, r)

    @pl.when(has_left)
    def _():
        greet(q - 2, r)

    greet(sibling, r)
    for step in range(1, n_res):
        greet(q, lax.rem(r + step, n_res))

    pl.semaphore_wait(
        barrier, n_res + has_right.astype(jnp.int32) + has_left.astype(jnp.int32)
    )

    grain = block // parts

    def pair_piece(source, p):
        start = source * block + p * grain
        return pair_all.at[pl.ds(pl.multiple_of(start, grain), grain), :]

    def pair_send_to(source_ref, source, p, way, target):
        return pltpu.make_async_remote_copy(
            src_ref=source_ref, dst_ref=pair_piece(source, p),
            send_sem=pair_send.at[way, source, p], recv_sem=pair_recv.at[source, p],
            device_id={"seq": target, "res": r}, device_id_type=MESH,
        )

    def own_sends(act):
        for p in range(parts):
            own = pair_in.at[pl.ds(p * grain, grain), :]

            @pl.when(has_right)
            def _():
                act(pair_send_to(own, q, p, 0, q + 2))

            @pl.when(has_left)
            def _():
                act(pair_send_to(own, q, p, 1, q - 2))

            act(pair_send_to(own, q, p, 2, sibling))

    def relay(d, p, first, act):
        lower = chip - d
        upper = chip + d

        @pl.when(lower >= 0)
        def _():
            source = lower * 2 + core
            first(source, p)

            @pl.when(has_right)
            def _():
                act(pair_send_to(pair_piece(source, p), source, p, 0, q + 2))

            act(pair_send_to(pair_piece(source, p), source, p, 2, sibling))

        @pl.when(upper < chips)
        def _():
            source = upper * 2 + core
            first(source, p)

            @pl.when(has_left)
            def _():
                act(pair_send_to(pair_piece(source, p), source, p, 1, q - 2))

            act(pair_send_to(pair_piece(source, p), source, p, 2, sibling))

    own_sends(lambda copy: copy.start())

    def left_send_to(step):
        return pltpu.make_async_remote_copy(
            src_ref=left_in, dst_ref=left_slot(r),
            send_sem=left_send.at[step], recv_sem=left_recv.at[r],
            device_id={"seq": q, "res": lax.rem(r + step, n_res)}, device_id_type=MESH,
        )

    for step in range(1, n_res):
        left_send_to(step).start()

    weight_copy.wait()
    weight_wide[...] = weight_raw[...].astype(jnp.float32)
    for e in range(width):
        weight_perm[e * width : (e + 1) * width, :] = weight_wide[
            pl.ds(e, width, stride=width), :
        ].astype(jnp.bfloat16)
    right_copy.wait()
    for b in range(lane_blocks):
        lanes = slice(b * LANES, (b + 1) * LANES)
        wide[b] = raw[:, lanes].astype(jnp.float32)
        for e in range(width):
            right_perm[e * n_right : (e + 1) * n_right, lanes] = wide[
                b, pl.ds(e, n_right, stride=width), :
            ].astype(jnp.bfloat16)
    right_acc[...] = jnp.zeros_like(right_acc)

    pair_copy.wait()

    def left_wait():
        left_copy.wait()
        for step in range(1, n_res):
            source = lax.rem(r + step, n_res)
            pltpu.make_async_copy(left_slot(source), left_slot(source), left_recv.at[source]).wait()

    def pair_wait(source, p):
        pltpu.make_async_copy(
            pair_piece(source, p), pair_piece(source, p), pair_recv.at[source, p]
        ).wait()

    def sum_send_to(index, owner):
        offset = lax.rem(index * piece, owned) * width
        return pltpu.make_async_remote_copy(
            src_ref=sum_send.at[pl.ds(pl.multiple_of(index * piece * width, piece * width), piece * width), :],
            dst_ref=sum_recv.at[r, pl.ds(pl.multiple_of(offset, piece * width), piece * width), :],
            send_sem=sum_send_sem.at[index], recv_sem=sum_recv_sem.at[r],
            device_id={"seq": q, "res": owner}, device_id_type=MESH,
        )

    pieces = chunk // piece
    group = max(1, 256 // n_right)
    group = math.gcd(group, chunk)
    span = group * n_right
    columns = width * n_right
    tile = math.gcd(columns, 512)

    halves = chunk // group

    def expand(which, s, low, high):
        for p in range(low, high):
            start = pl.multiple_of(which * (chunk * n_right) + p * span, span)
            grads = pair_all[pl.ds(start, span), :]
            expanded = lax.dot_general(
                weight_perm[...], grads, (((1,), (1,)), ((), ())), preferred_element_type=jnp.float32
            ).astype(jnp.bfloat16)
            for ii in range(group):
                i = p * group + ii
                for e in range(width):
                    outer[s, i * width : (i + 1) * width, e * n_right : (e + 1) * n_right] = expanded[
                        e * width : (e + 1) * width, ii * n_right : (ii + 1) * n_right
                    ]

    def stage_wait(which, s):
        for p in range(parts):
            pair_wait(which * 2 + (1 - core), p)
        expand(which, s, 0, halves // 2)

    def stage_expand(which, s):
        expand(which, s, halves // 2, halves)

    def stage_left(which, s):
        part = lax.dot_general(
            outer[s], right_perm[...], (((1,), (0,)), ((), ())), preferred_element_type=jnp.float32
        ) * inverse
        first = pl.multiple_of(which * (chunk * width), chunk * width)
        sum_send[pl.ds(first, chunk * width), :] = part.astype(jnp.bfloat16)
        for u in range(pieces):
            index = which * pieces + u
            owner = lax.div(index * piece, owned)

            @pl.when(owner == r)
            def _():
                offset = pl.multiple_of(lax.rem(index * piece, owned) * width, piece * width)
                sum_own[pl.ds(offset, piece * width), :] = part[
                    u * piece * width : (u + 1) * piece * width, :
                ]

            @pl.when(owner != r)
            def _():
                sum_send_to(index, owner).start()

    def stage_right(which, s):
        first = pl.multiple_of(which * (chunk * width), chunk * width)
        left_rows = left_all[pl.ds(first, chunk * width), :]
        for t in range(columns // tile):
            at = slice(t * tile, (t + 1) * tile)
            right_acc[:, at] += lax.dot_general(
                left_rows, outer[s, :, at], (((0,), (0,)), ((), ())), preferred_element_type=jnp.float32
            )

    stages = [stage_wait, stage_expand, stage_left, stage_right]

    def ring(d, carry):
        for p in range(parts):
            relay(d, p, pair_wait, lambda copy: copy.start())
            if p == parts - 1:
                pl.when(d == 1)(left_wait)
            todo = stages[p * len(stages) // parts : (p + 1) * len(stages) // parts]

            def side(s, inner):
                which = chip + (2 * s - 1) * (d - 1)

                @pl.when((which >= 0) & (which < chips) & ((d > 1) | (s == 0)))
                def _():
                    for stage in todo:
                        stage(which, s)

                return inner

            lax.fori_loop(0, 2, side, 0)
        return carry

    lax.fori_loop(1, chips + 1, ring, 0)

    for b in range(lane_blocks):
        lanes = slice(b * LANES, (b + 1) * LANES)
        for e in range(width):
            right_out[b, pl.ds(e, n_right, stride=width), :] = (
                jnp.transpose(right_acc[lanes, e * n_right : (e + 1) * n_right]) * inverse
            )
    total = sum_own[...]
    for step in range(1, n_res):
        source = lax.rem(r + step, n_res)
        pltpu.make_async_copy(sum_recv.at[source], sum_recv.at[source], sum_recv_sem.at[source]).wait()
        total = total + sum_recv[source].astype(jnp.float32)
    left_out[...] = total

    own_sends(lambda copy: copy.wait_send())

    def settle(d, carry):
        for p in range(parts):
            relay(d, p, lambda source, p: None, lambda copy: copy.wait_send())
        return carry

    lax.fori_loop(1, chips, settle, 0)
    for step in range(1, n_res):
        left_send_to(step).wait_send()

    def settle_sums(index, carry):
        owner = lax.div(index * piece, owned)

        @pl.when(owner != r)
        def _():
            sum_send_to(index, owner).wait_send()

        return carry

    lax.fori_loop(0, n_left // piece, settle_sums, 0)


def per_device(n_seq, n_res, pair_grad, out_weight, left_feat, right_feat):
    i_loc, n_right, pair = pair_grad.shape
    owned, width, rows = left_feat.shape
    n_left = n_seq * i_loc
    chunk = 2 * i_loc
    piece = math.gcd(chunk, owned)
    parts = math.gcd(i_loc, PARTS)
    sizes = (n_seq, n_res, i_loc, n_right, width, rows)
    lane_blocks = rows // LANES
    bf16, f32 = jnp.bfloat16, jnp.float32
    dma = pltpu.SemaphoreType.DMA
    grad_left, grad_right = pl.pallas_call(
        functools.partial(kernel, sizes),
        out_shape=(
            jax.ShapeDtypeStruct((owned * width, rows), f32),
            jax.ShapeDtypeStruct((lane_blocks, n_right * width, LANES), f32),
        ),
        in_specs=[pl.BlockSpec(memory_space=pltpu.HBM)] * 4,
        out_specs=(pl.BlockSpec(memory_space=pltpu.VMEM),) * 2,
        scratch_shapes=[
            pltpu.VMEM((n_left * n_right, pair), bf16),
            pltpu.VMEM((n_left * width, rows), bf16),
            pltpu.VMEM((n_res, owned * width, rows), bf16),
            pltpu.VMEM((n_left * width, rows), bf16),
            pltpu.VMEM((owned * width, rows), f32),
            pltpu.VMEM((n_right * width, rows), bf16),
            pltpu.VMEM((lane_blocks, n_right * width, LANES), f32),
            pltpu.VMEM((width * n_right, rows), bf16),
            pltpu.VMEM((width * width, pair), bf16),
            pltpu.VMEM((width * width, pair), f32),
            pltpu.VMEM((width * width, pair), bf16),
            pltpu.VMEM((2, chunk * width, width * n_right), bf16),
            pltpu.VMEM((rows, width * n_right), f32),
            dma((4,)),
            dma((n_seq, parts)),
            dma((3, n_seq, parts)),
            dma((n_res,)),
            dma((n_res,)),
            dma((n_res,)),
            dma((n_left // piece,)),
        ],
        compiler_params=pltpu.CompilerParams(
            collective_id=0, has_side_effects=True, vmem_limit_bytes=48 * 1024 * 1024
        ),
    )(
        *(
            pltpu.with_memory_space_constraint(x, pltpu.HBM)
            for x in (
                pair_grad.reshape(i_loc * n_right, pair),
                out_weight,
                left_feat.reshape(owned * width, rows),
                right_feat.reshape(n_right * width, rows),
            )
        )
    )
    return (
        grad_left.reshape(owned, width, rows),
        jnp.moveaxis(grad_right, 0, 1).reshape(n_right, width, rows),
    )


def solution(mesh):
    in_specs = (P("seq", "res", None), P(), P("res", None, "seq"), P("res", None, "seq"))
    out_specs = (P("res", None, "seq"), P("res", None, "seq"))
    body = functools.partial(per_device, mesh.shape["seq"], mesh.shape["res"])
    return jax.shard_map(body, mesh=mesh, in_specs=in_specs, out_specs=out_specs, check_vma=False)
```

```python
import functools
import math

import jax
import jax.numpy as jnp
from jax import lax
from jax.experimental import pallas as pl
from jax.experimental.pallas import tpu as pltpu
from jax.sharding import PartitionSpec as P

MESH = pl.DeviceIdType.MESH
LANES = 128
PARTS = 2


def kernel(
    sizes, pair_in, weight_in, left_in, right_in, left_out, right_out,
    pair_all, left_all, sum_recv, sum_send, sum_own, raw, wide, right_perm,
    weight_raw, weight_wide, weight_perm, outer, right_acc,
    local_sem, pair_recv, pair_send, left_recv, left_send, sum_recv_sem, sum_send_sem,
):
    n_seq, n_res, i_loc, n_right, width, rows = sizes
    chips = n_seq // 2
    parts = math.gcd(i_loc, PARTS)
    chunk = 2 * i_loc
    n_left = n_seq * i_loc
    owned = n_left // n_res
    piece = math.gcd(chunk, owned)
    inverse = 1.0 / (rows * n_seq)
    q = lax.axis_index("seq")
    r = lax.axis_index("res")
    core = lax.rem(q, 2)
    chip = lax.div(q, 2)
    sibling = chip * 2 + (1 - core)
    lane_blocks = rows // LANES

    block = i_loc * n_right
    share = owned * width

    def pair_slot(source):
        return pair_all.at[pl.ds(pl.multiple_of(source * block, block), block), :]

    def left_slot(source):
        return left_all.at[pl.ds(pl.multiple_of(source * share, share), share), :]

    weight_copy = pltpu.make_async_copy(weight_in, weight_raw, local_sem.at[0])
    weight_copy.start()
    right_copy = pltpu.make_async_copy(right_in, raw, local_sem.at[1])
    right_copy.start()
    left_copy = pltpu.make_async_copy(left_in, left_slot(r), local_sem.at[2])
    left_copy.start()
    pair_copy = pltpu.make_async_copy(pair_in, pair_slot(q), local_sem.at[3])
    pair_copy.start()

    barrier = pltpu.get_barrier_semaphore()

    def greet(seq, res):
        pl.semaphore_signal(
            barrier, inc=1, device_id={"seq": seq, "res": res}, device_id_type=MESH
        )

    has_right = chip < chips - 1
    has_left = chip > 0

    @pl.when(has_right)
    def _():
        greet(q + 2, r)

    @pl.when(has_left)
    def _():
        greet(q - 2, r)

    greet(sibling, r)
    for step in range(1, n_res):
        greet(q, lax.rem(r + step, n_res))

    pl.semaphore_wait(
        barrier, n_res + has_right.astype(jnp.int32) + has_left.astype(jnp.int32)
    )

    grain = block // parts

    def pair_piece(source, p):
        start = source * block + p * grain
        return pair_all.at[pl.ds(pl.multiple_of(start, grain), grain), :]

    def pair_send_to(source_ref, source, p, way, target):
        return pltpu.make_async_remote_copy(
            src_ref=source_ref, dst_ref=pair_piece(source, p),
            send_sem=pair_send.at[way, source, p], recv_sem=pair_recv.at[source, p],
            device_id={"seq": target, "res": r}, device_id_type=MESH,
        )

    def own_sends(act):
        for p in range(parts):
            own = pair_in.at[pl.ds(p * grain, grain), :]

            @pl.when(has_right)
            def _():
                act(pair_send_to(own, q, p, 0, q + 2))

            @pl.when(has_left)
            def _():
                act(pair_send_to(own, q, p, 1, q - 2))

            act(pair_send_to(own, q, p, 2, sibling))

    def relay(d, p, first, act):
        lower = chip - d
        upper = chip + d

        @pl.when(lower >= 0)
        def _():
            source = lower * 2 + core
            first(source, p)

            @pl.when(has_right)
            def _():
                act(pair_send_to(pair_piece(source, p), source, p, 0, q + 2))

            act(pair_send_to(pair_piece(source, p), source, p, 2, sibling))

        @pl.when(upper < chips)
        def _():
            source = upper * 2 + core
            first(source, p)

            @pl.when(has_left)
            def _():
                act(pair_send_to(pair_piece(source, p), source, p, 1, q - 2))

            act(pair_send_to(pair_piece(source, p), source, p, 2, sibling))

    own_sends(lambda copy: copy.start())

    def left_send_to(step):
        return pltpu.make_async_remote_copy(
            src_ref=left_in, dst_ref=left_slot(r),
            send_sem=left_send.at[step], recv_sem=left_recv.at[r],
            device_id={"seq": q, "res": lax.rem(r + step, n_res)}, device_id_type=MESH,
        )

    for step in range(1, n_res):
        left_send_to(step).start()

    weight_copy.wait()
    weight_wide[...] = weight_raw[...].astype(jnp.float32)
    for e in range(width):
        weight_perm[e * width : (e + 1) * width, :] = weight_wide[
            pl.ds(e, width, stride=width), :
        ].astype(jnp.bfloat16)
    right_copy.wait()
    for b in range(lane_blocks):
        lanes = slice(b * LANES, (b + 1) * LANES)
        wide[b] = raw[:, lanes].astype(jnp.float32)
        for e in range(width):
            right_perm[e * n_right : (e + 1) * n_right, lanes] = wide[
                b, pl.ds(e, n_right, stride=width), :
            ].astype(jnp.bfloat16)
    right_acc[...] = jnp.zeros_like(right_acc)

    pair_copy.wait()

    def left_wait():
        left_copy.wait()
        for step in range(1, n_res):
            source = lax.rem(r + step, n_res)
            pltpu.make_async_copy(left_slot(source), left_slot(source), left_recv.at[source]).wait()

    def pair_wait(source, p):
        pltpu.make_async_copy(
            pair_piece(source, p), pair_piece(source, p), pair_recv.at[source, p]
        ).wait()

    def sum_send_to(index, owner):
        offset = lax.rem(index * piece, owned) * width
        return pltpu.make_async_remote_copy(
            src_ref=sum_send.at[pl.ds(pl.multiple_of(index * piece * width, piece * width), piece * width), :],
            dst_ref=sum_recv.at[r, pl.ds(pl.multiple_of(offset, piece * width), piece * width), :],
            send_sem=sum_send_sem.at[index], recv_sem=sum_recv_sem.at[r],
            device_id={"seq": q, "res": owner}, device_id_type=MESH,
        )

    pieces = chunk // piece
    group = max(1, 256 // n_right)
    group = math.gcd(group, chunk)
    span = group * n_right
    columns = width * n_right
    tile = math.gcd(columns, 512)

    halves = chunk // group

    def expand(which, s, low, high):
        for p in range(low, high):
            start = pl.multiple_of(which * (chunk * n_right) + p * span, span)
            grads = pair_all[pl.ds(start, span), :]
            expanded = lax.dot_general(
                weight_perm[...], grads, (((1,), (1,)), ((), ())), preferred_element_type=jnp.float32
            ).astype(jnp.bfloat16)
            for ii in range(group):
                i = p * group + ii
                for e in range(width):
                    outer[s, i * width : (i + 1) * width, e * n_right : (e + 1) * n_right] = expanded[
                        e * width : (e + 1) * width, ii * n_right : (ii + 1) * n_right
                    ]

    def stage_wait(which, s):
        for p in range(parts):
            pair_wait(which * 2 + (1 - core), p)
        expand(which, s, 0, halves // 2)

    def stage_expand(which, s):
        expand(which, s, halves // 2, halves)

    def stage_left(which, s):
        part = lax.dot_general(
            outer[s], right_perm[...], (((1,), (0,)), ((), ())), preferred_element_type=jnp.float32
        ) * inverse
        first = pl.multiple_of(which * (chunk * width), chunk * width)
        sum_send[pl.ds(first, chunk * width), :] = part.astype(jnp.bfloat16)
        for u in range(pieces):
            index = which * pieces + u
            owner = lax.div(index * piece, owned)

            @pl.when(owner == r)
            def _():
                offset = pl.multiple_of(lax.rem(index * piece, owned) * width, piece * width)
                sum_own[pl.ds(offset, piece * width), :] = part[
                    u * piece * width : (u + 1) * piece * width, :
                ]

            @pl.when(owner != r)
            def _():
                sum_send_to(index, owner).start()

    def stage_right(which, s):
        first = pl.multiple_of(which * (chunk * width), chunk * width)
        left_rows = left_all[pl.ds(first, chunk * width), :]
        for t in range(columns // tile):
            at = slice(t * tile, (t + 1) * tile)
            right_acc[:, at] += lax.dot_general(
                left_rows, outer[s, :, at], (((0,), (0,)), ((), ())), preferred_element_type=jnp.float32
            )

    stages = [stage_wait, stage_expand, stage_left, stage_right]

    def ring(d, carry):
        for p in range(parts):
            relay(d, p, pair_wait, lambda copy: copy.start())
            if p == parts - 1:
                pl.when(d == 1)(left_wait)
            todo = stages if p == parts - 1 else []

            def side(s, inner):
                which = chip + (2 * s - 1) * (d - 1)

                @pl.when((which >= 0) & (which < chips) & ((d > 1) | (s == 0)))
                def _():
                    for stage in todo:
                        stage(which, s)

                return inner

            lax.fori_loop(0, 2, side, 0)
        return carry

    lax.fori_loop(1, chips + 1, ring, 0)

    for b in range(lane_blocks):
        lanes = slice(b * LANES, (b + 1) * LANES)
        for e in range(width):
            right_out[b, pl.ds(e, n_right, stride=width), :] = (
                jnp.transpose(right_acc[lanes, e * n_right : (e + 1) * n_right]) * inverse
            )
    total = sum_own[...]
    for step in range(1, n_res):
        source = lax.rem(r + step, n_res)
        pltpu.make_async_copy(sum_recv.at[source], sum_recv.at[source], sum_recv_sem.at[source]).wait()
        total = total + sum_recv[source].astype(jnp.float32)
    left_out[...] = total

    own_sends(lambda copy: copy.wait_send())

    def settle(d, carry):
        for p in range(parts):
            relay(d, p, lambda source, p: None, lambda copy: copy.wait_send())
        return carry

    lax.fori_loop(1, chips, settle, 0)
    for step in range(1, n_res):
        left_send_to(step).wait_send()

    def settle_sums(index, carry):
        owner = lax.div(index * piece, owned)

        @pl.when(owner != r)
        def _():
            sum_send_to(index, owner).wait_send()

        return carry

    lax.fori_loop(0, n_left // piece, settle_sums, 0)


def per_device(n_seq, n_res, pair_grad, out_weight, left_feat, right_feat):
    i_loc, n_right, pair = pair_grad.shape
    owned, width, rows = left_feat.shape
    n_left = n_seq * i_loc
    chunk = 2 * i_loc
    piece = math.gcd(chunk, owned)
    parts = math.gcd(i_loc, PARTS)
    sizes = (n_seq, n_res, i_loc, n_right, width, rows)
    lane_blocks = rows // LANES
    bf16, f32 = jnp.bfloat16, jnp.float32
    dma = pltpu.SemaphoreType.DMA
    grad_left, grad_right = pl.pallas_call(
        functools.partial(kernel, sizes),
        out_shape=(
            jax.ShapeDtypeStruct((owned * width, rows), f32),
            jax.ShapeDtypeStruct((lane_blocks, n_right * width, LANES), f32),
        ),
        in_specs=[pl.BlockSpec(memory_space=pltpu.HBM)] * 4,
        out_specs=(pl.BlockSpec(memory_space=pltpu.VMEM),) * 2,
        scratch_shapes=[
            pltpu.VMEM((n_left * n_right, pair), bf16),
            pltpu.VMEM((n_left * width, rows), bf16),
            pltpu.VMEM((n_res, owned * width, rows), bf16),
            pltpu.VMEM((n_left * width, rows), bf16),
            pltpu.VMEM((owned * width, rows), f32),
            pltpu.VMEM((n_right * width, rows), bf16),
            pltpu.VMEM((lane_blocks, n_right * width, LANES), f32),
            pltpu.VMEM((width * n_right, rows), bf16),
            pltpu.VMEM((width * width, pair), bf16),
            pltpu.VMEM((width * width, pair), f32),
            pltpu.VMEM((width * width, pair), bf16),
            pltpu.VMEM((2, chunk * width, width * n_right), bf16),
            pltpu.VMEM((rows, width * n_right), f32),
            dma((4,)),
            dma((n_seq, parts)),
            dma((3, n_seq, parts)),
            dma((n_res,)),
            dma((n_res,)),
            dma((n_res,)),
            dma((n_left // piece,)),
        ],
        compiler_params=pltpu.CompilerParams(
            collective_id=0, has_side_effects=True, vmem_limit_bytes=48 * 1024 * 1024
        ),
    )(
        *(
            pltpu.with_memory_space_constraint(x, pltpu.HBM)
            for x in (
                pair_grad.reshape(i_loc * n_right, pair),
                out_weight,
                left_feat.reshape(owned * width, rows),
                right_feat.reshape(n_right * width, rows),
            )
        )
    )
    return (
        grad_left.reshape(owned, width, rows),
        jnp.moveaxis(grad_right, 0, 1).reshape(n_right, width, rows),
    )


def solution(mesh):
    in_specs = (P("seq", "res", None), P(), P("res", None, "seq"), P("res", None, "seq"))
    out_specs = (P("res", None, "seq"), P("res", None, "seq"))
    body = functools.partial(per_device, mesh.shape["seq"], mesh.shape["res"])
    return jax.shard_map(body, mesh=mesh, in_specs=in_specs, out_specs=out_specs, check_vma=False)
```
